256 devices in a mesh: layer: 4 (over x), row: 8 (over y, core), col: 8 (over z).
Axes of the slice: x: 4, y: 4, z: 8, core: 2. Of those that a mesh axis runs over, the one named last changes fastest.
Arguments:
- left_values: bfloat16 [8192, 4, 2048], P('row', 'layer', 'col'), may hold values from -22 to 22
- left_pattern: int32 [32, 4, 8], P('row', 'layer', 'col'), may hold values from 0 to 1, as said below
- right_values: bfloat16 [8192, 4, 2048], P(('layer', 'row'), None, 'col'), may hold values from -6 to 6
- right_pattern: int32 [32, 4, 8], P(('layer', 'row'), None, 'col'), may hold values from 0 to 1, as said below
Outputs:
- expanded: bfloat16 [8192, 4, 2048], P('row', 'layer', 'col')
The draws below stay inside these ranges and needn't reach their ends.
Inputs may be any that keep to these rules, and one draw needn't show every extreme that they name: `left_pattern`: 1 marks a stored tile, 0 an absent one. `right_pattern`: 1 marks a stored tile, 0 an absent one.
All inputs are finite; a program needn't handle non-finite values.
Results may differ from the reference program's by a relative error of at most 0.001.
Values may be sent and summed in bfloat16 or wider, within the bound.
A program may use at most 64 MiB of HBM per device.

```python
import math
import jax
import jax.numpy as jnp

TILE = 256
N = 8192
N_LAYER = 4


def tile_pattern(key_base):
    tile_rows = N // TILE
    tile_cols = N // (N_LAYER * TILE)
    key_one, key_two = jax.random.split(key_base)
    density = jax.random.randint(key_one, (tile_rows, 1, 1), 20, 91)
    draws_int = jax.random.randint(key_two, (tile_rows, N_LAYER, tile_cols), 0, 100)
    return jnp.where(draws_int < density, 1, 0).astype(jnp.int32)


def draw_left_pattern(key, part):
    return tile_pattern(jax.random.fold_in(key, 11))


def draw_right_pattern(key, part):
    return tile_pattern(jax.random.fold_in(key, 23))


def draw_left_values(key, part):
    key_one, key_two = jax.random.split(jax.random.fold_in(key, 37), 2)
    shape_full = (N, N_LAYER, N // N_LAYER)
    position = jnp.arange(N, dtype=jnp.float32) / (N - 1)
    row_ramp = jnp.sqrt(1.0 + 2.0 * position)[:, None, None]
    spread = jnp.exp(jax.random.uniform(key_one, (N, 1, 1), jnp.float32) * math.log(math.sqrt(10.0)))
    sample = jnp.clip(jax.random.normal(key_two, shape_full, jnp.float32), -4.0, 4.0)
    return (sample * row_ramp * spread).astype(jnp.bfloat16)


def block_scale(stream_key, shape, shards, least, high):
    level = 1.0
    for dim, shards_of in shards:
        draws = jax.random.uniform(jax.random.fold_in(jax.random.fold_in(stream_key, 6), dim), (shards_of,), jnp.float32, least / len(shards), high / len(shards))
        level = level * jnp.repeat(jnp.exp(draws), shape[dim] // shards_of).reshape((-1,) + (1,) * (len(shape) - 1 - dim))
    return level


def noise(stream_key, extent, scale, bound, shards=(), held_as=jnp.bfloat16):
    loudness = block_scale(stream_key, extent, shards, -0.22, 0.18) if shards else 1.0
    result = jax.random.normal(stream_key, extent, jnp.float32) * scale * loudness
    return jnp.minimum(jnp.maximum(result, -bound), bound).astype(held_as)


def setup_inputs(seed: int = 0) -> dict:
    keys = jax.random.split(jax.random.key(seed), 5)
    return {
        "left_values": draw_left_values(jax.random.fold_in(keys[4], 71), 0),
        "left_pattern": draw_left_pattern(jax.random.fold_in(keys[4], 71), 0),
        "right_values": noise(keys[2], (N, N_LAYER, N // N_LAYER), 1.0, 6.0, ((0, 32), (2, 8))),
        "right_pattern": draw_right_pattern(jax.random.fold_in(keys[4], 71), 0),
    }


def expand_tiles(values, pattern):
    tile_rows, layers, tile_cols = pattern.shape
    tile_size = values.shape[0] // tile_rows
    blocks = values.reshape(tile_rows, tile_size, layers, tile_cols, tile_size)
    blocks = blocks * pattern[:, None, :, :, None].astype(values.dtype)
    return blocks.reshape(values.shape)


def reference(left_values, left_pattern, right_values, right_pattern):
    left_full = expand_tiles(left_values, left_pattern).reshape(N, N)
    right_full = expand_tiles(right_values, right_pattern).reshape(N, N)
    product = jnp.dot(left_full, right_full, preferred_element_type=jnp.float32)
    squared = product * product
    colmean = jnp.mean(squared, axis=0, keepdims=True)
    expanded = (squared / (colmean + 1e-6)).astype(jnp.bfloat16)
    return expanded.reshape(N, N_LAYER, N // N_LAYER)
```

```python
import jax
import jax.numpy as jnp
from jax import lax
from jax.sharding import PartitionSpec as P


def expand_tiles(values, pattern):
    tile_rows, layers, tile_cols = pattern.shape
    tile_size = values.shape[0] // tile_rows
    blocks = values.reshape(tile_rows, tile_size, layers, tile_cols, tile_size)
    blocks = blocks * pattern[:, None, :, :, None].astype(values.dtype)
    return blocks.reshape(values.shape)


def per_device(left_values, left_pattern, right_values, right_pattern):
    left_block = expand_tiles(left_values, left_pattern)
    right_block = expand_tiles(right_values, right_pattern)
    rows_local = left_block.shape[0]
    columns_local = left_block.shape[2]
    left_flat = left_block.reshape(rows_local, columns_local)
    right_flat = right_block.reshape(right_block.shape[0], -1)
    right_all = lax.all_gather(right_flat, "row", axis=0, tiled=True)
    left_all = lax.all_gather(left_flat, "col", axis=1, tiled=True)
    partial = jnp.dot(left_all, right_all, preferred_element_type=jnp.float32)
    layers = lax.axis_size("layer")
    partial = jnp.stack(
        [partial[:, columns_local * l : columns_local * (l + 1)] for l in range(layers)], axis=0
    )
    product = lax.psum_scatter(partial, "layer", scatter_dimension=0, tiled=True)
    product = product.reshape(rows_local, 1, columns_local)
    squared = product * product
    column = lax.psum(jnp.sum(squared, axis=0, keepdims=True), "row")
    rows_total = rows_local * lax.axis_size("row")
    colmean = column / rows_total
    return (squared / (colmean + 1e-06)).astype(jnp.bfloat16)


def solution(mesh):
    return jax.shard_map(
        per_device,
        mesh=mesh,
        in_specs=(
            P("row", "layer", "col"),
            P("row", "layer", "col"),
            P(("layer", "row"), None, "col"),
            P(("layer", "row"), None, "col"),
        ),
        out_specs=P("row", "layer", "col"),
        check_vma=False,
    )
```

```python
import functools

import jax
import jax.numpy as jnp
from jax import lax
from jax.experimental import pallas as pl
from jax.experimental.pallas import tpu as pltpu
from jax.sharding import PartitionSpec as P

MESH = pl.DeviceIdType.MESH
CHUNKS = 8
GROUPS = 2


def kernel(nl, nr, nz, lp, rp, lv, rv, out, lbuf, rbuf, part, recv_a, recv_b, recv_c, sq, sums, sums_all,
           zl_send, zl_recv, zs_send, zs_recv, y_send, y_recv, s_send, s_recv,
           a_send, a_recv, b_send, b_recv, c_send, c_recv, n_send, n_recv):
    x, r, z = lax.axis_index("layer"), lax.axis_index("row"), lax.axis_index("col")
    core = lax.rem(r, 2)
    sign = 1 - 2 * core
    tile = rv.shape[0]
    rows = lv.shape[0]
    cr = rows // CHUNKS
    gw = tile // GROUPS
    half = tile // 2

    def at_z(v):
        return lax.rem(v + 2 * nz, nz)

    def at_x(v):
        return lax.rem(v + 2 * nl, nl)

    def at_r(v):
        return lax.rem(v + 2 * nr, nr)

    sibling = r + sign
    barrier = pltpu.get_barrier_semaphore()
    peers = [(at_x(x + 1), r, z), (at_x(x - 1), r, z), (x, r, at_z(z + 1)), (x, r, at_z(z - 1))]
    peers += [(x, at_r(r + i), z) for i in range(1, nr)]
    for peer in peers:
        pl.semaphore_signal(barrier, inc=1, device_id=peer, device_id_type=MESH)

    for i in range(rows // tile):
        block = lv[pl.ds(i * tile, tile), :].astype(jnp.float32) * lp[i].astype(jnp.float32)
        lbuf[z, pl.ds(i * tile, tile), :] = block.astype(lbuf.dtype)
    for l in range(nl):
        block = (rv[:, l, :].astype(jnp.float32) * rp[l].astype(jnp.float32)).astype(rbuf.dtype)
        for g in range(GROUPS):
            rbuf[r, g, :, gw * l : gw * (l + 1)] = block[:, gw * g : gw * (g + 1)]
    pl.semaphore_wait(barrier, len(peers))

    def z_copy(h, c, long, receiving):
        d = sign if long else -sign
        owner = at_z(z - d * h) if receiving else at_z(z - d * (h - 1))
        ref = lbuf.at[owner, pl.ds(pl.multiple_of(c * cr, cr), cr), :]
        send, recv = (zl_send, zl_recv) if long else (zs_send, zs_recv)
        return pltpu.make_async_remote_copy(
            src_ref=ref, dst_ref=ref, send_sem=send.at[h - 1, c], recv_sem=recv.at[h - 1, c],
            device_id=(x, r, at_z(z + d)), device_id_type=MESH)

    def z_hop(h, c):
        if h > 1:
            z_copy(h - 1, c, True, True).wait_recv()
        if h <= nz // 2:
            z_copy(h, c, True, False).start()
        if h > 1 and h <= nz // 2:
            z_copy(h - 1, c, False, True).wait_recv()
        if h < nz // 2:
            z_copy(h, c, False, False).start()

    def z_step(t):
        for h in range(1, nz // 2 + 2):
            c = t - (h - 1)
            if isinstance(t, int):
                if 0 <= c < CHUNKS:
                    z_hop(h, c)
            else:
                pl.when(c < CHUNKS)(functools.partial(z_hop, h, c))

    def y_copy(g, i, up, hop, receiving):
        d = 2 if up else -2
        owner = at_r(r - d * hop) if receiving else at_r(r - d * (hop - 1))
        ref = rbuf.at[owner, g, pl.ds(half * i, half), :]
        n = 2 if hop == 2 else (0 if up else 1)
        return pltpu.make_async_remote_copy(
            src_ref=ref, dst_ref=ref, send_sem=y_send.at[g, i, n], recv_sem=y_recv.at[g, i, n],
            device_id=(x, at_r(r + d), z), device_id_type=MESH)

    def s_copy(g, i, n, owner):
        ref = rbuf.at[owner, g, pl.ds(half * i, half), :]
        return pltpu.make_async_remote_copy(
            src_ref=ref, dst_ref=ref, send_sem=s_send.at[g, i, n], recv_sem=s_recv.at[g, i, n],
            device_id=(x, sibling, z), device_id_type=MESH)

    def y_own(g):
        y_copy(g, 0, True, 1, False).start()
        y_copy(g, 1, False, 1, False).start()
        y_copy(g, 1, True, 1, False).start()
        y_copy(g, 0, False, 1, False).start()
        s_copy(g, 0, 3, r).start()
        s_copy(g, 1, 3, r).start()

    def y_first(g):
        for i in (0, 1):
            up = i == 0
            y_copy(g, i, up, 1, True).wait_recv()
            y_copy(g, i, up, 2, False).start()
            s_copy(g, i, 0 if up else 1, at_r(r - 2 if up else r + 2)).start()

    def y_second(g):
        for i in (1, 0):
            up = i == 1
            y_copy(g, i, up, 1, True).wait_recv()
            s_copy(g, i, 0 if up else 1, at_r(r - 2 if up else r + 2)).start()

    def y_third(g):
        for i in (0, 1):
            y_copy(g, i, i == 0, 2, True).wait_recv()
            s_copy(g, i, 2, at_r(r + 4)).start()

    def y_ready(g):
        for i in (0, 1):
            for n, o in ((3, 0), (0, -2), (1, 2), (2, 4)):
                s_copy(g, i, n, at_r(sibling + o)).wait_recv()

    def cell(w):
        first = 1 - lax.min(w // 6, 1)
        c = first * lax.rem(w, 3) + (1 - first) * (w // 2)
        g = first * (w // 3) + (1 - first) * lax.rem(w, 2)
        return g, pl.ds(pl.multiple_of(c * cr, cr), cr)

    def a_copy(w):
        g, rs = cell(w)
        return pltpu.make_async_remote_copy(
            src_ref=part.at[at_x(x + 2), g, rs, :], dst_ref=recv_a.at[g, rs, :], send_sem=a_send.at[w],
            recv_sem=a_recv.at[w], device_id=(at_x(x + sign), r, z), device_id_type=MESH)

    def c_copy(w):
        g, rs = cell(w)
        return pltpu.make_async_remote_copy(
            src_ref=part.at[at_x(x - sign), g, rs, :], dst_ref=recv_c.at[g, rs, :], send_sem=c_send.at[w],
            recv_sem=c_recv.at[w], device_id=(at_x(x - sign), r, z), device_id_type=MESH)

    def b_copy(w):
        g, rs = cell(w)
        return pltpu.make_async_remote_copy(
            src_ref=part.at[at_x(x + sign), g, rs, :], dst_ref=recv_b.at[g, rs, :], send_sem=b_send.at[w],
            recv_sem=b_recv.at[w], device_id=(at_x(x + sign), r, z), device_id_type=MESH)

    items = CHUNKS * GROUPS

    def multiply(w):
        g, rs = cell(w)
        acc = jnp.dot(lbuf[0, rs, :], rbuf[0, g], preferred_element_type=jnp.float32)
        for j in range(1, nz):
            acc += jnp.dot(lbuf[j, rs, :], rbuf[j, g], preferred_element_type=jnp.float32)
        for l in range(nl):
            part[l, g, rs, :] = acc[:, gw * l : gw * (l + 1)]

    def add_first(w):
        g, rs = cell(w)
        a_copy(w).wait_recv()
        part[at_x(x + sign), g, rs, :] += recv_a[g, rs, :]

    def finish(w):
        g, rs = cell(w)
        c_copy(w).wait_recv()
        b_copy(w).wait_recv()
        total = part[x, g, rs, :] + recv_c[g, rs, :] + recv_b[g, rs, :]
        square = total * total
        sq[g, rs, :] = square
        sums[g] += jnp.sum(square.reshape(cr // 8, 8, gw), axis=0)

    sums[...] = jnp.zeros_like(sums)
    z_step(0)
    y_own(0)
    y_own(1)
    z_step(1)
    z_step(2)
    y_first(0)
    y_second(0)
    z_step(3)
    y_third(0)
    y_ready(0)

    def body(w, _):
        for w0, t in ((0, 4), (1, 5), (2, 6), (5, 7)):
            pl.when(w == w0)(functools.partial(z_step, t))

        @pl.when((w == 0))
        def _():
            y_first(1)

        @pl.when((w == 1))
        def _():
            y_second(1)
            y_third(1)

        @pl.when((w == 3))
        def _():
            y_ready(1)

        @pl.when((w >= 8) & (lax.rem(w, 2) == 0) & (w < items))
        def _():
            z_step(w // 2 + 4)

        @pl.when((w >= 2) & (w < items + 2))
        def _():
            add_first(w - 2)

        @pl.when(w < items)
        def _():
            multiply(w)

        @pl.when((w >= 2) & (w < items + 2))
        def _():
            b_copy(w - 2).start()

        @pl.when(w < items)
        def _():
            a_copy(w).start()
            c_copy(w).start()

        @pl.when(w >= 4)
        def _():
            finish(w - 4)

        return 0

    lax.fori_loop(0, items + 4, body, 0)

    def n_copy(i, receiving):
        slot = at_r(r - i) if receiving else r
        ref = sums_all.at[slot]
        return pltpu.make_async_remote_copy(
            src_ref=ref, dst_ref=ref, send_sem=n_send.at[i], recv_sem=n_recv.at[i],
            device_id=(x, at_r(r + i), z), device_id_type=MESH)

    sums_all[r] = sums[...]
    for i in range(1, nr):
        n_copy(i, False).start()

    def drain(w, _):
        a_copy(w).wait_send()
        b_copy(w).wait_send()
        c_copy(w).wait_send()
        return 0

    lax.fori_loop(0, items, drain, 0)

    def drain_z(c, _):
        for h in range(1, nz // 2 + 1):
            z_copy(h, c, True, False).wait_send()
            if h < nz // 2:
                z_copy(h, c, False, False).wait_send()
        return 0

    lax.fori_loop(0, CHUNKS, drain_z, 0)
    for g in range(GROUPS):
        for i in (0, 1):
            for up in (True, False):
                y_copy(g, i, up, 1, False).wait_send()
            y_copy(g, i, i == 0, 2, False).wait_send()
            for n in range(4):
                s_copy(g, i, n, r).wait_send()

    for i in range(1, nr):
        n_copy(i, True).wait_recv()
    total = sums_all[0]
    for i in range(1, nr):
        total += sums_all[i]
    scale = 1.0 / (jnp.sum(total, axis=1, keepdims=True) * (1.0 / (rows * nr)) + 1e-6)
    for g in range(GROUPS):
        out[:, gw * g : gw * (g + 1)] = (sq[g] * scale[g]).astype(out.dtype)
    for i in range(1, nr):
        n_copy(i, False).wait_send()


def per_device(nl, nr, nz, left_values, left_pattern, right_values, right_pattern):
    rows, _, tile = left_values.shape
    f32, bf16 = jnp.float32, jnp.bfloat16
    gw = tile // GROUPS
    items = CHUNKS * GROUPS
    dma = pltpu.SemaphoreType.DMA
    smem, vmem = pl.BlockSpec(memory_space=pltpu.SMEM), pl.BlockSpec(memory_space=pltpu.VMEM)
    out = pl.pallas_call(
        functools.partial(kernel, nl, nr, nz),
        out_shape=jax.ShapeDtypeStruct((rows, tile), bf16),
        in_specs=[smem, smem, vmem, vmem],
        out_specs=vmem,
        scratch_shapes=[
            pltpu.VMEM((nz, rows, tile), bf16),
            pltpu.VMEM((nr, GROUPS, tile, nl * gw), bf16),
            pltpu.VMEM((nl, GROUPS, rows, gw), f32),
            pltpu.VMEM((GROUPS, rows, gw), f32),
            pltpu.VMEM((GROUPS, rows, gw), f32),
            pltpu.VMEM((GROUPS, rows, gw), f32),
            pltpu.VMEM((GROUPS, rows, gw), f32),
            pltpu.VMEM((GROUPS, 8, gw), f32),
            pltpu.VMEM((nr, GROUPS, 8, gw), f32),
            dma((nz // 2, CHUNKS)), dma((nz // 2, CHUNKS)),
            dma((nz // 2, CHUNKS)), dma((nz // 2, CHUNKS)),
            dma((GROUPS, 2, 3)), dma((GROUPS, 2, 3)),
            dma((GROUPS, 2, 4)), dma((GROUPS, 2, 4)),
            dma((items,)), dma((items,)), dma((items,)), dma((items,)), dma((items,)), dma((items,)),
            dma((nr,)), dma((nr,)),
        ],
        compiler_params=pltpu.CompilerParams(
            collective_id=0, has_side_effects=True, vmem_limit_bytes=40 * 1024 * 1024),
    )(left_pattern.reshape(-1), right_pattern.reshape(-1), left_values.reshape(rows, tile), right_values)
    return out.reshape(rows, 1, tile)


def solution(mesh):
    sizes = mesh.shape["layer"], mesh.shape["row"], mesh.shape["col"]
    return jax.shard_map(
        functools.partial(per_device, *sizes),
        mesh=mesh,
        in_specs=(
            P("row", "layer", "col"),
            P("row", "layer", "col"),
            P(("layer", "row"), None, "col"),
            P(("layer", "row"), None, "col"),
        ),
        out_specs=P("row", "layer", "col"),
        check_vma=False,
    )
```

```python
import functools

import jax
import jax.numpy as jnp
from jax import lax
from jax.experimental import pallas as pl
from jax.experimental.pallas import tpu as pltpu
from jax.sharding import PartitionSpec as P

MESH = pl.DeviceIdType.MESH
CHUNKS = 16
LEAD = 1
LAG = 4
GROUPS = 2


def kernel(nl, nr, nz, lp, rp, lv_hbm, rv_hbm, out, lv, rv, lbuf, rbuf, part, recv_a, recv_b, recv_c, sq, sums, sums_all,
           zl_send, zl_recv, zs_send, zs_recv, y_send, y_recv, s_send, s_recv,
           a_send, a_recv, b_send, b_recv, c_send, c_recv, n_send, n_recv, in_sem):
    x, r, z = lax.axis_index("layer"), lax.axis_index("row"), lax.axis_index("col")
    core = lax.rem(r, 2)
    sign = 1 - 2 * core
    tile = rv.shape[0]
    rows = lv.shape[0]
    cr = rows // CHUNKS
    gw = tile // GROUPS
    half = tile // 2

    def at_z(v):
        return lax.rem(v + 2 * nz, nz)

    def at_x(v):
        return lax.rem(v + 2 * nl, nl)

    def at_r(v):
        return lax.rem(v + 2 * nr, nr)

    sibling = r + sign
    barrier = pltpu.get_barrier_semaphore()
    peers = [(at_x(x + 1), r, z), (at_x(x - 1), r, z), (x, r, at_z(z + 1)), (x, r, at_z(z - 1))]
    peers += [(x, at_r(r + i), z) for i in range(1, nr)]
    fetch_left = pltpu.make_async_copy(lv_hbm, lv, in_sem.at[0])
    fetch_right = pltpu.make_async_copy(rv_hbm, rv, in_sem.at[1])
    fetch_left.start()
    fetch_right.start()
    for peer in peers:
        pl.semaphore_signal(barrier, inc=1, device_id=peer, device_id_type=MESH)

    fetch_left.wait()
    for i in range(rows // tile):
        block = lv[pl.ds(i * tile, tile), :].astype(jnp.float32) * lp[i].astype(jnp.float32)
        lbuf[z, pl.ds(i * tile, tile), :] = block.astype(lbuf.dtype)
    fetch_right.wait()
    for l in range(nl):
        block = (rv[:, l, :].astype(jnp.float32) * rp[l].astype(jnp.float32)).astype(rbuf.dtype)
        for g in range(GROUPS):
            rbuf[r, g, :, gw * l : gw * (l + 1)] = block[:, gw * g : gw * (g + 1)]
    pl.semaphore_wait(barrier, len(peers))

    def z_copy(h, c, long, receiving):
        d = sign if long else -sign
        owner = at_z(z - d * h) if receiving else at_z(z - d * (h - 1))
        ref = lbuf.at[owner, pl.ds(pl.multiple_of(c * cr, cr), cr), :]
        send, recv = (zl_send, zl_recv) if long else (zs_send, zs_recv)
        return pltpu.make_async_remote_copy(
            src_ref=ref, dst_ref=ref, send_sem=send.at[h - 1, c], recv_sem=recv.at[h - 1, c],
            device_id=(x, r, at_z(z + d)), device_id_type=MESH)

    def z_hop(h, c):
        if h > 1:
            z_copy(h - 1, c, True, True).wait_recv()
        if h <= nz // 2:
            z_copy(h, c, True, False).start()
        if h > 1 and h <= nz // 2:
            z_copy(h - 1, c, False, True).wait_recv()
        if h < nz // 2:
            z_copy(h, c, False, False).start()

    def z_tick(n, odd):
        for h in range(nz // 2 + 1, 0, -1):
            delay = 3 * (h - 1) if h > 1 else -2 * LEAD
            if delay % 2 != odd:
                continue
            if isinstance(n, int):
                c = (n - delay) // 2
                if 0 <= c < CHUNKS:
                    z_hop(h, c)
            else:
                c = (n - delay) // 2
                pl.when(c < CHUNKS)(functools.partial(z_hop, h, c))

    def y_copy(g, i, up, hop, receiving):
        d = 2 if up else -2
        owner = at_r(r - d * hop) if receiving else at_r(r - d * (hop - 1))
        ref = rbuf.at[owner, g, pl.ds(half * i, half), :]
        n = 2 if hop == 2 else (0 if up else 1)
        return pltpu.make_async_remote_copy(
            src_ref=ref, dst_ref=ref, send_sem=y_send.at[g, i, n], recv_sem=y_recv.at[g, i, n],
            device_id=(x, at_r(r + d), z), device_id_type=MESH)

    def s_copy(g, i, n, owner):
        ref = rbuf.at[owner, g, pl.ds(half * i, half), :]
        return pltpu.make_async_remote_copy(
            src_ref=ref, dst_ref=ref, send_sem=s_send.at[g, i, n], recv_sem=s_recv.at[g, i, n],
            device_id=(x, sibling, z), device_id_type=MESH)

    def y_own(g):
        y_copy(g, 0, True, 1, False).start()
        y_copy(g, 1, False, 1, False).start()
        y_copy(g, 1, True, 1, False).start()
        y_copy(g, 0, False, 1, False).start()
        s_copy(g, 0, 3, r).start()
        s_copy(g, 1, 3, r).start()

    def y_first(g):
        for i in (0, 1):
            up = i == 0
            y_copy(g, i, up, 1, True).wait_recv()
            y_copy(g, i, up, 2, False).start()
            s_copy(g, i, 0 if up else 1, at_r(r - 2 if up else r + 2)).start()
        if g + 1 < GROUPS:
            y_own(g + 1)

    def y_second(g):
        for i in (1, 0):
            up = i == 1
            y_copy(g, i, up, 1, True).wait_recv()
            s_copy(g, i, 0 if up else 1, at_r(r - 2 if up else r + 2)).start()

    def y_third(g):
        for i in (0, 1):
            y_copy(g, i, i == 0, 2, True).wait_recv()
            s_copy(g, i, 2, at_r(r + 4)).start()

    def y_ready(g):
        for i in (0, 1):
            for n, o in ((3, 0), (0, -2), (1, 2), (2, 4)):
                s_copy(g, i, n, at_r(sibling + o)).wait_recv()

    def cell(w):
        late = lax.min(w // 5, 1)
        q, s = lax.max(w - 5, 0) // 5, lax.rem(w, 5)
        odd = lax.rem(s, 2)
        c = (1 - late) * w + late * (odd * (5 + 2 * q) + (1 - odd) * 3 * q + s // 2)
        g = late * (1 - odd)
        return g, pl.ds(pl.multiple_of(c * cr, cr), cr)

    def a_copy(w):
        g, rs = cell(w)
        return pltpu.make_async_remote_copy(
            src_ref=part.at[at_x(x + 2), g, rs, :], dst_ref=recv_a.at[g, rs, :], send_sem=a_send.at[w],
            recv_sem=a_recv.at[w], device_id=(at_x(x + sign), r, z), device_id_type=MESH)

    def c_copy(w):
        g, rs = cell(w)
        return pltpu.make_async_remote_copy(
            src_ref=part.at[at_x(x - sign), g, rs, :], dst_ref=recv_c.at[g, rs, :], send_sem=c_send.at[w],
            recv_sem=c_recv.at[w], device_id=(at_x(x - sign), r, z), device_id_type=MESH)

    def b_copy(w):
        g, rs = cell(w)
        return pltpu.make_async_remote_copy(
            src_ref=part.at[at_x(x + sign), g, rs, :], dst_ref=recv_b.at[g, rs, :], send_sem=b_send.at[w],
            recv_sem=b_recv.at[w], device_id=(at_x(x + sign), r, z), device_id_type=MESH)

    items = CHUNKS * GROUPS

    def multiply(w):
        g, rs = cell(w)
        acc = jnp.dot(lbuf[0, rs, :], rbuf[0, g], preferred_element_type=jnp.float32)
        for j in range(1, nz):
            acc += jnp.dot(lbuf[j, rs, :], rbuf[j, g], preferred_element_type=jnp.float32)
        for l in range(nl):
            part[l, g, rs, :] = acc[:, gw * l : gw * (l + 1)]

    def add_first(w):
        g, rs = cell(w)
        a_copy(w).wait_recv()
        part[at_x(x + sign), g, rs, :] += recv_a[g, rs, :]

    def finish(w):
        g, rs = cell(w)
        c_copy(w).wait_recv()
        b_copy(w).wait_recv()
        total = part[x, g, rs, :] + recv_c[g, rs, :] + recv_b[g, rs, :]
        square = total * total
        sq[g, rs, :] = square
        sums[g] += jnp.sum(square.reshape(cr // 8, 8, gw), axis=0)

    def item(w, _):
        @pl.when((w >= LAG) & (w < items + LAG))
        def _():
            add_first(w - LAG)

        @pl.when(w < items)
        def _():
            multiply(w)

        @pl.when((w >= LAG) & (w < items + LAG))
        def _():
            b_copy(w - LAG).start()

        @pl.when(w < items)
        def _():
            a_copy(w).start()
            c_copy(w).start()

        @pl.when(w >= 2 * LAG)
        def _():
            finish(w - 2 * LAG)

        return 0

    def done(n):
        early = lax.max(lax.min(lax.min(n - 13, (n - 10) // 2), 5), 0)
        late = (lax.max(n - 20, 0) * 5) // 4
        return lax.min(early + late, items - 2 + (2 * LAG + 2) * (n // 42))

    sums[...] = jnp.zeros_like(sums)
    for c in range(LEAD):
        z_hop(1, c)
    z_tick(0, 0)
    y_own(0)
    for n in range(1, 12):
        z_tick(n, n % 2)
        if n == 6:
            y_first(0)
        if n == 9:
            y_second(0)

    def tick(n, _):
        pl.when(lax.rem(n, 2) == 0)(functools.partial(z_tick, n, 0))
        pl.when(lax.rem(n, 2) == 1)(functools.partial(z_tick, n, 1))
        for n0, f, g in ((12, y_third, 0), (14, y_ready, 0), (15, y_first, 1), (17, y_second, 1), (19, y_third, 1), (21, y_ready, 1)):
            pl.when(n == n0)(functools.partial(f, g))
        lax.fori_loop(done(n - 1), done(n), item, 0)
        return 0

    lax.fori_loop(12, 50, tick, 0)

    def n_copy(i, receiving):
        slot = at_r(r - i) if receiving else r
        ref = sums_all.at[slot]
        return pltpu.make_async_remote_copy(
            src_ref=ref, dst_ref=ref, send_sem=n_send.at[i], recv_sem=n_recv.at[i],
            device_id=(x, at_r(r + i), z), device_id_type=MESH)

    for g in range(GROUPS):
        sums_all[r, :, gw * g : gw * (g + 1)] = jnp.sum(sums[g], axis=0, keepdims=True)
    for i in range(1, nr):
        n_copy(i, False).start()

    def drain(w, _):
        a_copy(w).wait_send()
        b_copy(w).wait_send()
        c_copy(w).wait_send()
        return 0

    lax.fori_loop(0, items, drain, 0)

    def drain_z(c, _):
        for h in range(1, nz // 2 + 1):
            z_copy(h, c, True, False).wait_send()
            if h < nz // 2:
                z_copy(h, c, False, False).wait_send()
        return 0

    lax.fori_loop(0, CHUNKS, drain_z, 0)
    for g in range(GROUPS):
        for i in (0, 1):
            for up in (True, False):
                y_copy(g, i, up, 1, False).wait_send()
            y_copy(g, i, i == 0, 2, False).wait_send()
            for n in range(4):
                s_copy(g, i, n, r).wait_send()

    for i in range(1, nr):
        n_copy(i, True).wait_recv()
    total = sums_all[0]
    for i in range(1, nr):
        total += sums_all[i]
    scale = 1.0 / (total * (1.0 / (rows * nr)) + 1e-6)
    for g in range(GROUPS):
        cols = slice(gw * g, gw * (g + 1))
        out[:, cols] = (sq[g] * scale[:, cols]).astype(out.dtype)
    for i in range(1, nr):
        n_copy(i, False).wait_send()


def per_device(nl, nr, nz, left_values, left_pattern, right_values, right_pattern):
    rows, _, tile = left_values.shape
    f32, bf16 = jnp.float32, jnp.bfloat16
    gw = tile // GROUPS
    items = CHUNKS * GROUPS
    dma = pltpu.SemaphoreType.DMA
    smem, vmem = pl.BlockSpec(memory_space=pltpu.SMEM), pl.BlockSpec(memory_space=pltpu.VMEM)
    hbm = pl.BlockSpec(memory_space=pltpu.HBM)
    out = pl.pallas_call(
        functools.partial(kernel, nl, nr, nz),
        out_shape=jax.ShapeDtypeStruct((rows, tile), bf16),
        in_specs=[smem, smem, hbm, hbm],
        out_specs=vmem,
        scratch_shapes=[
            pltpu.VMEM((rows, tile), bf16),
            pltpu.VMEM(right_values.shape, bf16),
            pltpu.VMEM((nz, rows, tile), bf16),
            pltpu.VMEM((nr, GROUPS, tile, nl * gw), bf16),
            pltpu.VMEM((nl, GROUPS, rows, gw), f32),
            pltpu.VMEM((GROUPS, rows, gw), f32),
            pltpu.VMEM((GROUPS, rows, gw), f32),
            pltpu.VMEM((GROUPS, rows, gw), f32),
            pltpu.VMEM((GROUPS, rows, gw), f32),
            pltpu.VMEM((GROUPS, 8, gw), f32),
            pltpu.VMEM((nr, 1, tile), f32),
            dma((nz // 2, CHUNKS)), dma((nz // 2, CHUNKS)),
            dma((nz // 2, CHUNKS)), dma((nz // 2, CHUNKS)),
            dma((GROUPS, 2, 3)), dma((GROUPS, 2, 3)),
            dma((GROUPS, 2, 4)), dma((GROUPS, 2, 4)),
            dma((items,)), dma((items,)), dma((items,)), dma((items,)), dma((items,)), dma((items,)),
            dma((nr,)), dma((nr,)), dma((2,)),
        ],
        compiler_params=pltpu.CompilerParams(
            collective_id=0, has_side_effects=True, vmem_limit_bytes=40 * 1024 * 1024),
    )(left_pattern.reshape(-1), right_pattern.reshape(-1), left_values.reshape(rows, tile), right_values)
    return out.reshape(rows, 1, tile)


def solution(mesh):
    sizes = mesh.shape["layer"], mesh.shape["row"], mesh.shape["col"]
    return jax.shard_map(
        functools.partial(per_device, *sizes),
        mesh=mesh,
        in_specs=(
            P("row", "layer", "col"),
            P("row", "layer", "col"),
            P(("layer", "row"), None, "col"),
            P(("layer", "row"), None, "col"),
        ),
        out_specs=P("row", "layer", "col"),
        check_vma=False,
    )
```

```python
import functools

import jax
import jax.numpy as jnp
from jax import lax
from jax.experimental import pallas as pl
from jax.experimental.pallas import tpu as pltpu
from jax.sharding import PartitionSpec as P

MESH = pl.DeviceIdType.MESH
CHUNKS = 16
LEAD = 1
LAG = 6
GROUPS = 2


def kernel(nl, nr, nz, lp, rp, lv_hbm, rv_hbm, out, lv, rv, lbuf, rbuf, part, recv_a, recv_b, recv_c, sq, sums, sums_all,
           zl_send, zl_recv, zs_send, zs_recv, y_send, y_recv, s_send, s_recv,
           a_send, a_recv, b_send, b_recv, c_send, c_recv, n_send, n_recv, in_sem):
    x, r, z = lax.axis_index("layer"), lax.axis_index("row"), lax.axis_index("col")
    core = lax.rem(r, 2)
    sign = 1 - 2 * core
    tile = rv.shape[0]
    rows = lv.shape[0]
    cr = rows // CHUNKS
    gw = tile // GROUPS
    half = tile // 2

    def at_z(v):
        return lax.rem(v + 2 * nz, nz)

    def at_x(v):
        return lax.rem(v + 2 * nl, nl)

    def at_r(v):
        return lax.rem(v + 2 * nr, nr)

    sibling = r + sign
    barrier = pltpu.get_barrier_semaphore()
    peers = [(at_x(x + 1), r, z), (at_x(x - 1), r, z), (x, r, at_z(z + 1)), (x, r, at_z(z - 1))]
    peers += [(x, at_r(r + i), z) for i in range(1, nr)]
    fetch_left = pltpu.make_async_copy(lv_hbm, lv, in_sem.at[0])
    fetch_right = pltpu.make_async_copy(rv_hbm, rv, in_sem.at[1])
    fetch_left.start()
    fetch_right.start()
    for peer in peers:
        pl.semaphore_signal(barrier, inc=1, device_id=peer, device_id_type=MESH)

    fetch_left.wait()
    for i in range(rows // tile):
        block = lv[pl.ds(i * tile, tile), :].astype(jnp.float32) * lp[i].astype(jnp.float32)
        lbuf[z, pl.ds(i * tile, tile), :] = block.astype(lbuf.dtype)
    pl.semaphore_wait(barrier, len(peers))

    def z_copy(h, c, long, receiving):
        d = sign if long else -sign
        owner = at_z(z - d * h) if receiving else at_z(z - d * (h - 1))
        ref = lbuf.at[owner, pl.ds(pl.multiple_of(c * cr, cr), cr), :]
        send, recv = (zl_send, zl_recv) if long else (zs_send, zs_recv)
        return pltpu.make_async_remote_copy(
            src_ref=ref, dst_ref=ref, send_sem=send.at[h - 1, c], recv_sem=recv.at[h - 1, c],
            device_id=(x, r, at_z(z + d)), device_id_type=MESH)

    def z_hop(h, c):
        if h > 1:
            z_copy(h - 1, c, True, True).wait_recv()
        if h <= nz // 2:
            z_copy(h, c, True, False).start()
        if h > 1 and h <= nz // 2:
            z_copy(h - 1, c, False, True).wait_recv()
        if h < nz // 2:
            z_copy(h, c, False, False).start()

    def z_tick(n, odd):
        for h in range(nz // 2 + 1, 0, -1):
            delay = 3 * (h - 1) if h > 1 else -2 * LEAD
            if delay % 2 != odd:
                continue
            if isinstance(n, int):
                c = (n - delay) // 2
                if 0 <= c < CHUNKS:
                    z_hop(h, c)
            else:
                c = (n - delay) // 2
                pl.when((c >= 0) & (c < CHUNKS))(functools.partial(z_hop, h, c))

    def y_copy(g, i, up, hop, receiving):
        d = 2 if up else -2
        owner = at_r(r - d * hop) if receiving else at_r(r - d * (hop - 1))
        ref = rbuf.at[owner, g, pl.ds(half * i, half), :]
        n = 2 if hop == 2 else (0 if up else 1)
        return pltpu.make_async_remote_copy(
            src_ref=ref, dst_ref=ref, send_sem=y_send.at[g, i, n], recv_sem=y_recv.at[g, i, n],
            device_id=(x, at_r(r + d), z), device_id_type=MESH)

    def s_copy(g, i, n, owner):
        ref = rbuf.at[owner, g, pl.ds(half * i, half), :]
        return pltpu.make_async_remote_copy(
            src_ref=ref, dst_ref=ref, send_sem=s_send.at[g, i, n], recv_sem=s_recv.at[g, i, n],
            device_id=(x, sibling, z), device_id_type=MESH)

    def y_own(g):
        y_copy(g, 0, True, 1, False).start()
        y_copy(g, 1, False, 1, False).start()
        y_copy(g, 1, True, 1, False).start()
        y_copy(g, 0, False, 1, False).start()
        s_copy(g, 0, 3, r).start()
        s_copy(g, 1, 3, r).start()

    def y_first(g):
        for i in (0, 1):
            up = i == 0
            y_copy(g, i, up, 1, True).wait_recv()
            y_copy(g, i, up, 2, False).start()
            s_copy(g, i, 0 if up else 1, at_r(r - 2 if up else r + 2)).start()
        if g + 1 < GROUPS:
            y_own(g + 1)

    def y_second(g):
        for i in (1, 0):
            up = i == 1
            y_copy(g, i, up, 1, True).wait_recv()
            s_copy(g, i, 0 if up else 1, at_r(r - 2 if up else r + 2)).start()

    def y_third(g):
        for i in (0, 1):
            y_copy(g, i, i == 0, 2, True).wait_recv()
            s_copy(g, i, 2, at_r(r + 4)).start()

    def y_ready(g):
        for i in (0, 1):
            for n, o in ((3, 0), (0, -2), (1, 2), (2, 4)):
                s_copy(g, i, n, at_r(sibling + o)).wait_recv()

    def cell(w):
        late = lax.min(w // 5, 1)
        q, s = lax.max(w - 5, 0) // 5, lax.rem(w, 5)
        odd = lax.rem(s, 2)
        c = (1 - late) * w + late * (odd * (5 + 2 * q) + (1 - odd) * 3 * q + s // 2)
        g = late * (1 - odd)
        return g, pl.ds(pl.multiple_of(c * cr, cr), cr)

    def a_copy(w):
        g, rs = cell(w)
        return pltpu.make_async_remote_copy(
            src_ref=part.at[at_x(x + 2), g, rs, :], dst_ref=recv_a.at[g, rs, :], send_sem=a_send.at[w],
            recv_sem=a_recv.at[w], device_id=(at_x(x + sign), r, z), device_id_type=MESH)

    def c_copy(w):
        g, rs = cell(w)
        return pltpu.make_async_remote_copy(
            src_ref=part.at[at_x(x - sign), g, rs, :], dst_ref=recv_c.at[g, rs, :], send_sem=c_send.at[w],
            recv_sem=c_recv.at[w], device_id=(at_x(x - sign), r, z), device_id_type=MESH)

    def b_copy(w):
        g, rs = cell(w)
        return pltpu.make_async_remote_copy(
            src_ref=part.at[at_x(x + sign), g, rs, :], dst_ref=recv_b.at[g, rs, :], send_sem=b_send.at[w],
            recv_sem=b_recv.at[w], device_id=(at_x(x + sign), r, z), device_id_type=MESH)

    items = CHUNKS * GROUPS

    def multiply(w):
        g, rs = cell(w)
        acc = jnp.dot(lbuf[0, rs, :], rbuf[0, g], preferred_element_type=jnp.float32)
        for j in range(1, nz):
            acc += jnp.dot(lbuf[j, rs, :], rbuf[j, g], preferred_element_type=jnp.float32)
        for l in range(nl):
            part[l, g, rs, :] = acc[:, gw * l : gw * (l + 1)]

    def add_first(w):
        g, rs = cell(w)
        a_copy(w).wait_recv()
        part[at_x(x + sign), g, rs, :] += recv_a[g, rs, :]

    def finish(w):
        g, rs = cell(w)
        c_copy(w).wait_recv()
        b_copy(w).wait_recv()
        total = part[x, g, rs, :] + recv_c[g, rs, :] + recv_b[g, rs, :]
        square = total * total
        sq[g, rs, :] = square
        sums[g] += jnp.sum(square.reshape(cr // 8, 8, gw), axis=0)

    def item(w, _):
        @pl.when((w >= LAG) & (w < items + LAG))
        def _():
            add_first(w - LAG)

        @pl.when(w < items)
        def _():
            multiply(w)

        @pl.when((w >= LAG) & (w < items + LAG))
        def _():
            b_copy(w - LAG).start()

        @pl.when(w < items)
        def _():
            a_copy(w).start()
            c_copy(w).start()

        @pl.when(w >= 2 * LAG)
        def _():
            finish(w - 2 * LAG)

        return 0

    def done(n):
        early = lax.max(lax.min(lax.min(n - 13, (n - 10) // 2), 5), 0)
        late = (lax.max(n - 20, 0) * 5) // 4 + 3 * LAG * (n // 43)
        return lax.min(early + late, items - 2 + (2 * LAG + 2) * (n // 42))

    sums[...] = jnp.zeros_like(sums)
    for c in range(LEAD):
        z_hop(1, c)
    z_tick(0, 0)
    fetch_right.wait()
    for l in range(nl):
        block = (rv[:, l, :].astype(jnp.float32) * rp[l].astype(jnp.float32)).astype(rbuf.dtype)
        for g in range(GROUPS):
            rbuf[r, g, :, gw * l : gw * (l + 1)] = block[:, gw * g : gw * (g + 1)]
    y_own(0)
    for n in range(1, 12):
        z_tick(n, n % 2)
        if n == 6:
            y_first(0)
        if n == 9:
            y_second(0)

    def tick(n, _):
        pl.when(lax.rem(n, 2) == 0)(functools.partial(z_tick, n, 0))
        pl.when(lax.rem(n, 2) == 1)(functools.partial(z_tick, n, 1))
        for n0, f, g in ((12, y_third, 0), (14, y_ready, 0), (15, y_first, 1), (17, y_second, 1), (19, y_third, 1), (21, y_ready, 1)):
            pl.when(n == n0)(functools.partial(f, g))
        lax.fori_loop(done(n - 1), done(n), item, 0)
        return 0

    lax.fori_loop(12, 50, tick, 0)

    def n_copy(i, receiving):
        slot = at_r(r - i) if receiving else r
        ref = sums_all.at[slot]
        return pltpu.make_async_remote_copy(
            src_ref=ref, dst_ref=ref, send_sem=n_send.at[i], recv_sem=n_recv.at[i],
            device_id=(x, at_r(r + i), z), device_id_type=MESH)

    for g in range(GROUPS):
        sums_all[r, :, gw * g : gw * (g + 1)] = jnp.sum(sums[g], axis=0, keepdims=True)
    for i in range(1, nr):
        n_copy(i, False).start()

    def drain(w, _):
        a_copy(w).wait_send()
        b_copy(w).wait_send()
        c_copy(w).wait_send()
        return 0

    lax.fori_loop(0, items, drain, 0)

    def drain_z(c, _):
        for h in range(1, nz // 2 + 1):
            z_copy(h, c, True, False).wait_send()
            if h < nz // 2:
                z_copy(h, c, False, False).wait_send()
        return 0

    lax.fori_loop(0, CHUNKS, drain_z, 0)
    for g in range(GROUPS):
        for i in (0, 1):
            for up in (True, False):
                y_copy(g, i, up, 1, False).wait_send()
            y_copy(g, i, i == 0, 2, False).wait_send()
            for n in range(4):
                s_copy(g, i, n, r).wait_send()

    for i in range(1, nr):
        n_copy(i, True).wait_recv()
    total = sums_all[0]
    for i in range(1, nr):
        total += sums_all[i]
    scale = 1.0 / (total * (1.0 / (rows * nr)) + 1e-6)
    for g in range(GROUPS):
        cols = slice(gw * g, gw * (g + 1))
        out[:, cols] = (sq[g] * scale[:, cols]).astype(out.dtype)
    for i in range(1, nr):
        n_copy(i, False).wait_send()


def per_device(nl, nr, nz, left_values, left_pattern, right_values, right_pattern):
    rows, _, tile = left_values.shape
    f32, bf16 = jnp.float32, jnp.bfloat16
    gw = tile // GROUPS
    items = CHUNKS * GROUPS
    dma = pltpu.SemaphoreType.DMA
    smem, vmem = pl.BlockSpec(memory_space=pltpu.SMEM), pl.BlockSpec(memory_space=pltpu.VMEM)
    hbm = pl.BlockSpec(memory_space=pltpu.HBM)
    out = pl.pallas_call(
        functools.partial(kernel, nl, nr, nz),
        out_shape=jax.ShapeDtypeStruct((rows, tile), bf16),
        in_specs=[smem, smem, hbm, hbm],
        out_specs=vmem,
        scratch_shapes=[
            pltpu.VMEM((rows, tile), bf16),
            pltpu.VMEM(right_values.shape, bf16),
            pltpu.VMEM((nz, rows, tile), bf16),
            pltpu.VMEM((nr, GROUPS, tile, nl * gw), bf16),
            pltpu.VMEM((nl, GROUPS, rows, gw), f32),
            pltpu.VMEM((GROUPS, rows, gw), f32),
            pltpu.VMEM((GROUPS, rows, gw), f32),
            pltpu.VMEM((GROUPS, rows, gw), f32),
            pltpu.VMEM((GROUPS, rows, gw), f32),
            pltpu.VMEM((GROUPS, 8, gw), f32),
            pltpu.VMEM((nr, 1, tile), f32),
            dma((nz // 2, CHUNKS)), dma((nz // 2, CHUNKS)),
            dma((nz // 2, CHUNKS)), dma((nz // 2, CHUNKS)),
            dma((GROUPS, 2, 3)), dma((GROUPS, 2, 3)),
            dma((GROUPS, 2, 4)), dma((GROUPS, 2, 4)),
            dma((items,)), dma((items,)), dma((items,)), dma((items,)), dma((items,)), dma((items,)),
            dma((nr,)), dma((nr,)), dma((2,)),
        ],
        compiler_params=pltpu.CompilerParams(
            collective_id=0, has_side_effects=True, vmem_limit_bytes=66000000),
    )(left_pattern.reshape(-1), right_pattern.reshape(-1), left_values.reshape(rows, tile), right_values)
    return out.reshape(rows, 1, tile)


def solution(mesh):
    sizes = mesh.shape["layer"], mesh.shape["row"], mesh.shape["col"]
    return jax.shard_map(
        functools.partial(per_device, *sizes),
        mesh=mesh,
        in_specs=(
            P("row", "layer", "col"),
            P("row", "layer", "col"),
            P(("layer", "row"), None, "col"),
            P(("layer", "row"), None, "col"),
        ),
        out_specs=P("row", "layer", "col"),
        check_vma=False,
    )
```

```python
import functools

import jax
import jax.numpy as jnp
from jax import lax
from jax.experimental import pallas as pl
from jax.experimental.pallas import tpu as pltpu
from jax.sharding import PartitionSpec as P

MESH = pl.DeviceIdType.MESH
CHUNKS = 16
LEAD = 1
LAG = 6
GROUPS = 2


def kernel(nl, nr, nz, lp, rp, lv_hbm, rv_hbm, out, lv, rv, lbuf, rbuf, part, recv_a, recv_b, recv_c, sq, sums, sums_all,
           zl_send, zl_recv, zs_send, zs_recv, y_send, y_recv, s_send, s_recv,
           a_send, a_recv, b_send, b_recv, c_send, c_recv, n_send, n_recv, in_sem):
    x, r, z = lax.axis_index("layer"), lax.axis_index("row"), lax.axis_index("col")
    core = lax.rem(r, 2)
    sign = 1 - 2 * core
    tile = rv.shape[0]
    rows = lv.shape[0]
    cr = rows // CHUNKS
    gw = tile // GROUPS
    half = tile // 2

    def at_z(v):
        return lax.rem(v + 2 * nz, nz)

    def at_x(v):
        return lax.rem(v + 2 * nl, nl)

    def at_r(v):
        return lax.rem(v + 2 * nr, nr)

    sibling = r + sign
    barrier = pltpu.get_barrier_semaphore()
    peers = [(at_x(x + 1), r, z), (at_x(x - 1), r, z), (x, r, at_z(z + 1)), (x, r, at_z(z - 1))]
    peers += [(x, at_r(r + i), z) for i in range(1, nr)]
    fetch_left = pltpu.make_async_copy(lv_hbm, lv, in_sem.at[0])
    fetch_right = pltpu.make_async_copy(rv_hbm, rv, in_sem.at[1])
    fetch_left.start()
    fetch_right.start()
    for peer in peers:
        pl.semaphore_signal(barrier, inc=1, device_id=peer, device_id_type=MESH)

    fetch_left.wait()
    for i in range(rows // tile):
        block = lv[pl.ds(i * tile, tile), :].astype(jnp.float32) * lp[i].astype(jnp.float32)
        lbuf[z, pl.ds(i * tile, tile), :] = block.astype(lbuf.dtype)
    pl.semaphore_wait(barrier, len(peers))

    def z_copy(h, c, long, receiving):
        d = sign if long else -sign
        owner = at_z(z - d * h) if receiving else at_z(z - d * (h - 1))
        ref = lbuf.at[owner, pl.ds(pl.multiple_of(c * cr, cr), cr), :]
        send, recv = (zl_send, zl_recv) if long else (zs_send, zs_recv)
        return pltpu.make_async_remote_copy(
            src_ref=ref, dst_ref=ref, send_sem=send.at[h - 1, c], recv_sem=recv.at[h - 1, c],
            device_id=(x, r, at_z(z + d)), device_id_type=MESH)

    def z_hop(h, c):
        if h > 1:
            z_copy(h - 1, c, True, True).wait_recv()
        if h <= nz // 2:
            z_copy(h, c, True, False).start()
        if h > 1 and h <= nz // 2:
            z_copy(h - 1, c, False, True).wait_recv()
        if h < nz // 2:
            z_copy(h, c, False, False).start()

    def z_tick(n, odd):
        for h in range(nz // 2 + 1, 0, -1):
            delay = 3 * (h - 1) if h > 1 else -2 * LEAD
            if delay % 2 != odd:
                continue
            if isinstance(n, int):
                c = (n - delay) // 2
                if 0 <= c < CHUNKS:
                    z_hop(h, c)
            else:
                c = (n - delay) // 2
                pl.when((c >= 0) & (c < CHUNKS))(functools.partial(z_hop, h, c))

    def y_copy(g, i, up, hop, receiving):
        d = 2 if up else -2
        owner = at_r(r - d * hop) if receiving else at_r(r - d * (hop - 1))
        ref = rbuf.at[owner, g, pl.ds(half * i, half), :]
        n = 2 if hop == 2 else (0 if up else 1)
        return pltpu.make_async_remote_copy(
            src_ref=ref, dst_ref=ref, send_sem=y_send.at[g, i, n], recv_sem=y_recv.at[g, i, n],
            device_id=(x, at_r(r + d), z), device_id_type=MESH)

    def s_copy(g, i, n, owner):
        ref = rbuf.at[owner, g, pl.ds(half * i, half), :]
        return pltpu.make_async_remote_copy(
            src_ref=ref, dst_ref=ref, send_sem=s_send.at[g, i, n], recv_sem=s_recv.at[g, i, n],
            device_id=(x, sibling, z), device_id_type=MESH)

    def y_own(g):
        y_copy(g, 0, True, 1, False).start()
        y_copy(g, 1, False, 1, False).start()
        y_copy(g, 1, True, 1, False).start()
        y_copy(g, 0, False, 1, False).start()
        s_copy(g, 0, 3, r).start()
        s_copy(g, 1, 3, r).start()

    def y_first(g):
        for i in (0, 1):
            up = i == 0
            y_copy(g, i, up, 1, True).wait_recv()
            y_copy(g, i, up, 2, False).start()
            s_copy(g, i, 0 if up else 1, at_r(r - 2 if up else r + 2)).start()
        if g + 1 < GROUPS:
            y_own(g + 1)

    def y_second(g):
        for i in (1, 0):
            up = i == 1
            y_copy(g, i, up, 1, True).wait_recv()
            s_copy(g, i, 0 if up else 1, at_r(r - 2 if up else r + 2)).start()

    def y_third(g):
        for i in (0, 1):
            y_copy(g, i, i == 0, 2, True).wait_recv()
            s_copy(g, i, 2, at_r(r + 4)).start()

    def y_ready(g):
        for i in (0, 1):
            for n, o in ((3, 0), (0, -2), (1, 2), (2, 4)):
                s_copy(g, i, n, at_r(sibling + o)).wait_recv()

    def cell(w):
        late = lax.min(w // 5, 1)
        q, s = lax.max(w - 5, 0) // 5, lax.rem(w, 5)
        odd = lax.rem(s, 2)
        c = (1 - late) * w + late * (odd * (5 + 2 * q) + (1 - odd) * 3 * q + s // 2)
        g = late * (1 - odd)
        return g, pl.ds(pl.multiple_of(c * cr, cr), cr)

    def a_copy(w):
        g, rs = cell(w)
        return pltpu.make_async_remote_copy(
            src_ref=part.at[at_x(x + 2), g, rs, :], dst_ref=recv_a.at[g, rs, :], send_sem=a_send.at[w],
            recv_sem=a_recv.at[w], device_id=(at_x(x + sign), r, z), device_id_type=MESH)

    def c_copy(w):
        g, rs = cell(w)
        return pltpu.make_async_remote_copy(
            src_ref=part.at[at_x(x - sign), g, rs, :], dst_ref=recv_c.at[g, rs, :], send_sem=c_send.at[w],
            recv_sem=c_recv.at[w], device_id=(at_x(x - sign), r, z), device_id_type=MESH)

    def b_copy(w):
        g, rs = cell(w)
        return pltpu.make_async_remote_copy(
            src_ref=part.at[at_x(x + sign), g, rs, :], dst_ref=recv_b.at[g, rs, :], send_sem=b_send.at[w],
            recv_sem=b_recv.at[w], device_id=(at_x(x + sign), r, z), device_id_type=MESH)

    items = CHUNKS * GROUPS

    def multiply(w):
        g, rs = cell(w)
        acc = jnp.dot(lbuf[0, rs, :], rbuf[0, g], preferred_element_type=jnp.float32)
        for j in range(1, nz):
            acc += jnp.dot(lbuf[j, rs, :], rbuf[j, g], preferred_element_type=jnp.float32)
        for l in range(nl):
            part[l, g, rs, :] = acc[:, gw * l : gw * (l + 1)]

    def add_first(w):
        g, rs = cell(w)
        a_copy(w).wait_recv()
        part[at_x(x + sign), g, rs, :] += recv_a[g, rs, :]

    def finish(w):
        g, rs = cell(w)
        c_copy(w).wait_recv()
        b_copy(w).wait_recv()
        total = part[x, g, rs, :] + recv_c[g, rs, :] + recv_b[g, rs, :]
        square = total * total
        sq[g, rs, :] = square
        sums[g] += jnp.sum(square.reshape(cr // 8, 8, gw), axis=0)

    def item(w, _):
        @pl.when(w < items)
        def _():
            multiply(w)
            a_copy(w).start()
            c_copy(w).start()

        @pl.when((w >= LAG) & (w < items + LAG))
        def _():
            add_first(w - LAG)
            b_copy(w - LAG).start()

        @pl.when(w >= 2 * LAG)
        def _():
            finish(w - 2 * LAG)

        return 0

    def done(n):
        early = lax.max(lax.min(lax.min(n - 13, (n - 10) // 2), 5), 0)
        late = (lax.max(n - 20, 0) * 5) // 4 + 3 * LAG * (n // 43)
        return lax.min(early + late, items - 2 + (2 * LAG + 2) * (n // 42))

    sums[...] = jnp.zeros_like(sums)
    for c in range(LEAD):
        z_hop(1, c)
    z_tick(0, 0)
    fetch_right.wait()
    for l in range(nl):
        block = (rv[:, l, :].astype(jnp.float32) * rp[l].astype(jnp.float32)).astype(rbuf.dtype)
        for g in range(GROUPS):
            rbuf[r, g, :, gw * l : gw * (l + 1)] = block[:, gw * g : gw * (g + 1)]
    y_own(0)
    for n in range(1, 12):
        z_tick(n, n % 2)
        if n == 6:
            y_first(0)
        if n == 9:
            y_second(0)

    def tick(n, _):
        pl.when(lax.rem(n, 2) == 0)(functools.partial(z_tick, n, 0))
        pl.when(lax.rem(n, 2) == 1)(functools.partial(z_tick, n, 1))
        for n0, f, g in ((12, y_third, 0), (14, y_ready, 0), (15, y_first, 1), (17, y_second, 1), (19, y_third, 1), (21, y_ready, 1)):
            pl.when(n == n0)(functools.partial(f, g))
        lax.fori_loop(done(n - 1), done(n), item, 0)
        return 0

    lax.fori_loop(12, 50, tick, 0)

    def n_copy(i, receiving):
        slot = at_r(r - i) if receiving else r
        ref = sums_all.at[slot]
        return pltpu.make_async_remote_copy(
            src_ref=ref, dst_ref=ref, send_sem=n_send.at[i], recv_sem=n_recv.at[i],
            device_id=(x, at_r(r + i), z), device_id_type=MESH)

    for g in range(GROUPS):
        sums_all[r, :, gw * g : gw * (g + 1)] = jnp.sum(sums[g], axis=0, keepdims=True)
    for i in range(1, nr):
        n_copy(i, False).start()

    def drain(w, _):
        a_copy(w).wait_send()
        b_copy(w).wait_send()
        c_copy(w).wait_send()
        return 0

    lax.fori_loop(0, items, drain, 0)

    def drain_z(c, _):
        for h in range(1, nz // 2 + 1):
            z_copy(h, c, True, False).wait_send()
            if h < nz // 2:
                z_copy(h, c, False, False).wait_send()
        return 0

    lax.fori_loop(0, CHUNKS, drain_z, 0)
    for g in range(GROUPS):
        for i in (0, 1):
            for up in (True, False):
                y_copy(g, i, up, 1, False).wait_send()
            y_copy(g, i, i == 0, 2, False).wait_send()
            for n in range(4):
                s_copy(g, i, n, r).wait_send()

    for i in range(1, nr):
        n_copy(i, True).wait_recv()
    total = sums_all[0]
    for i in range(1, nr):
        total += sums_all[i]
    scale = 1.0 / (total * (1.0 / (rows * nr)) + 1e-6)
    for g in range(GROUPS):
        cols = slice(gw * g, gw * (g + 1))
        out[:, cols] = (sq[g] * scale[:, cols]).astype(out.dtype)
    for i in range(1, nr):
        n_copy(i, False).wait_send()


def per_device(nl, nr, nz, left_values, left_pattern, right_values, right_pattern):
    rows, _, tile = left_values.shape
    f32, bf16 = jnp.float32, jnp.bfloat16
    gw = tile // GROUPS
    items = CHUNKS * GROUPS
    dma = pltpu.SemaphoreType.DMA
    smem, vmem = pl.BlockSpec(memory_space=pltpu.SMEM), pl.BlockSpec(memory_space=pltpu.VMEM)
    hbm = pl.BlockSpec(memory_space=pltpu.HBM)
    out = pl.pallas_call(
        functools.partial(kernel, nl, nr, nz),
        out_shape=jax.ShapeDtypeStruct((rows, tile), bf16),
        in_specs=[smem, smem, hbm, hbm],
        out_specs=vmem,
        scratch_shapes=[
            pltpu.VMEM((rows, tile), bf16),
            pltpu.VMEM(right_values.shape, bf16),
            pltpu.VMEM((nz, rows, tile), bf16),
            pltpu.VMEM((nr, GROUPS, tile, nl * gw), bf16),
            pltpu.VMEM((nl, GROUPS, rows, gw), f32),
            pltpu.VMEM((GROUPS, rows, gw), f32),
            pltpu.VMEM((GROUPS, rows, gw), f32),
            pltpu.VMEM((GROUPS, rows, gw), f32),
            pltpu.VMEM((GROUPS, rows, gw), f32),
            pltpu.VMEM((GROUPS, 8, gw), f32),
            pltpu.VMEM((nr, 1, tile), f32),
            dma((nz // 2, CHUNKS)), dma((nz // 2, CHUNKS)),
            dma((nz // 2, CHUNKS)), dma((nz // 2, CHUNKS)),
            dma((GROUPS, 2, 3)), dma((GROUPS, 2, 3)),
            dma((GROUPS, 2, 4)), dma((GROUPS, 2, 4)),
            dma((items,)), dma((items,)), dma((items,)), dma((items,)), dma((items,)), dma((items,)),
            dma((nr,)), dma((nr,)), dma((2,)),
        ],
        compiler_params=pltpu.CompilerParams(
            collective_id=0, has_side_effects=True, vmem_limit_bytes=66000000),
    )(left_pattern.reshape(-1), right_pattern.reshape(-1), left_values.reshape(rows, tile), right_values)
    return out.reshape(rows, 1, tile)


def solution(mesh):
    sizes = mesh.shape["layer"], mesh.shape["row"], mesh.shape["col"]
    return jax.shard_map(
        functools.partial(per_device, *sizes),
        mesh=mesh,
        in_specs=(
            P("row", "layer", "col"),
            P("row", "layer", "col"),
            P(("layer", "row"), None, "col"),
            P(("layer", "row"), None, "col"),
        ),
        out_specs=P("row", "layer", "col"),
        check_vma=False,
    )
```
